512 devices in a mesh: line: 32 (over x, y, core), seg: 16 (over z).
Axes of the slice: x: 4, y: 4, z: 16, core: 2. Of those that a mesh axis runs over, the one named last changes fastest.
Arguments:
- points: float32 [32, 16, 3, 32768], P('line', 'seg'), may hold values from -1 to 1
- rows: int32 [32, 16, 2, 3072], P('line', 'seg'), may hold values from -1 to 32767, as said below
- cells: int32 [32, 16, 2, 24], P('line', 'seg'), may hold values from -1 to 15, as said below
- pose: float32 [12, 32], P(None, 'line'), as said below
Outputs:
- matched: float32 [32, 16, 2, 5, 3072], P('line', 'seg')
- fitted_pose: float32 [12, 32], P(None, 'line')
- final_spread: float32 [1], replicated
The draws below stay inside these ranges and needn't reach their ends.
Inputs may be any that keep to these rules, and one draw needn't show every extreme that they name: In each block of 128 slots the filled slots come first; every slot of an empty block is empty; rows toward the lower line lie in the lower margin (below 8192), rows toward the upper line in the upper margin (24576 or more); the lists of line 0 toward the lower side and of line 32 - 1 toward the upper side are empty. `cells`: empty blocks come after the others; in segment 0 of every line all blocks toward an existing adjacent line are filled. `pose`: every 3x3 part is within about 0.5 of the identity.
All inputs are finite; a program needn't handle non-finite values.
Results may differ from the reference program's by a relative error of at most 0.0003.
Values sent between devices are 32-bit elements; how exact they have to be, the bound alone decides.
A program may use at most 64 MiB of HBM per device.

```python
import jax
import jax.numpy as jnp
from jax import lax

NCELL = 16
CT = 512
NPTS = 32768
NBLK = 24
BLOCK = 128
ITERS = 2
SLOTS = 3072
LINES = 32
SEGS = 16


def route_tables(key):
    margin = NCELL * CT
    base = jax.random.fold_in(key, 11)
    key_count, key_cell, key_fill, key_rows = jax.random.split(base, 4)
    block_count = jax.random.randint(key_count, (LINES, SEGS, 2, 1), NBLK // 3, NBLK + 1)
    seg_index = jnp.arange(SEGS).reshape(1, SEGS, 1, 1)
    block_count = jnp.where(seg_index == 0, NBLK, block_count)
    line_index = jnp.arange(LINES).reshape(LINES, 1, 1, 1)
    side_index = jnp.arange(2).reshape(1, 1, 2, 1)
    edge_lists = (line_index == 0) & (side_index == 0) | (line_index == LINES - 1) & (side_index == 1)
    block_index = jnp.arange(NBLK).reshape(1, 1, 1, NBLK)
    live_blocks = (block_index < block_count) & jnp.logical_not(edge_lists)
    cell_draw = jax.random.randint(key_cell, (LINES, SEGS, 2, NBLK), 0, NCELL)
    top_cell = (line_index == 0) & (seg_index == 0) & (side_index == 1) & (block_index == 0)
    cell_draw = jnp.where(top_cell, NCELL - 1, cell_draw)
    cell_ids = jnp.where(live_blocks, cell_draw, -1).astype(jnp.int32)
    fill_count = jax.random.randint(key_fill, (LINES, SEGS, 2, NBLK, 1), 32, BLOCK + 1)
    slot_index = jnp.arange(BLOCK).reshape(1, 1, 1, 1, BLOCK)
    slot_live = (slot_index < fill_count) & live_blocks[..., None]
    row_draw = jax.random.randint(key_rows, (LINES, SEGS, 2, NBLK, BLOCK), 0, margin)
    side_full = jnp.arange(2).reshape(1, 1, 2, 1, 1)
    row_draw = jnp.where(side_full == 1, row_draw + (NPTS - margin), row_draw)
    top_row = top_cell[..., None] & (slot_index == 0)
    row_draw = jnp.where(top_row, NPTS - 1, row_draw)
    row_ids = jnp.where(slot_live, row_draw, -1).reshape(LINES, SEGS, 2, NBLK * BLOCK).astype(jnp.int32)
    return (row_ids, cell_ids)


def draw_rows(key, part):
    return route_tables(key)[0]


def draw_cells(key, part):
    return route_tables(key)[1]


def draw_pose(key, part):
    noise = jax.random.normal(jax.random.fold_in(key, 5), (12, LINES), jnp.float32)
    scales = jnp.array([0.1] * 9 + [0.2] * 3, jnp.float32)[:, None]
    identity = jnp.array([1, 0, 0, 0, 1, 0, 0, 0, 1, 0, 0, 0], jnp.float32)[:, None]
    return identity + scales * noise


def levels(rng, dims, shards, smallest, top_value):
    factor_of, own = 1.0, jax.random.fold_in(rng, 6)
    for position, shards_of in shards:
        draws = jnp.exp(jax.random.uniform(jax.random.fold_in(own, position), (shards_of,), jnp.float32, smallest / len(shards), top_value / len(shards)))
        factor_of = factor_of * jnp.repeat(draws, dims[position] // shards_of).reshape([-1 if axis == position else 1 for axis in range(len(dims))])
    return factor_of


def setup_inputs(seed: int = 0) -> dict:
    streams_of = jax.random.split(jax.random.key(seed), 5)
    points = jnp.clip(jax.random.uniform(streams_of[0], (LINES, SEGS, 3, NPTS), jnp.float32, -1.0, 1.0) * levels(streams_of[0], (LINES, SEGS, 3, NPTS), ((0, 32), (1, 16)), -0.4, 0.0), -1.0, 1.0)
    rows = draw_rows(jax.random.fold_in(streams_of[4], 71), 0)
    cells = draw_cells(jax.random.fold_in(streams_of[4], 71), 0)
    pose = draw_pose(jax.random.fold_in(streams_of[4], 71), 0)
    return dict(points=points, rows=rows, cells=cells, pose=pose)


OUTLIER_MASS = 1.0
SPREAD_START = 0.05
PRIOR_TOP = 0.05
PRIOR_BOTTOM = 1.0
REGULARIZE = 1.0

def match_block(source_block, cell_id, world_points, spread):
    first_column = (jnp.maximum(cell_id, 0) * CT).astype(jnp.int32)
    target = lax.dynamic_slice_in_dim(world_points, first_column, CT, 1)
    distance = (source_block[0][:, None] - target[0][None, :]) ** 2
    distance = distance + (source_block[1][:, None] - target[1][None, :]) ** 2
    distance = distance + (source_block[2][:, None] - target[2][None, :]) ** 2
    weight = jnp.exp(-distance / (2.0 * spread))
    total_weight = jnp.sum(weight, axis=1)
    posterior = weight / (total_weight + OUTLIER_MASS)[:, None]
    pulled = lax.dot_general(target.astype(jnp.float32), posterior.astype(jnp.float32), (((1,), (1,)), ((), ())), precision=lax.Precision.HIGHEST, preferred_element_type=jnp.float32)
    share_row = total_weight / (total_weight + OUTLIER_MASS)
    energy_row = jnp.sum(posterior * distance, axis=1)
    merged_rows = jnp.concatenate([pulled, share_row[None, :], energy_row[None, :]], axis=0)
    return jnp.where(cell_id >= 0, merged_rows, jnp.zeros_like(merged_rows))

def solve_pose(gram_matrix, cross_matrix, pose_column):
    old_pose = jnp.concatenate([pose_column[:9].reshape(3, 3), pose_column[9:].reshape(3, 1)], axis=1)
    left_side = gram_matrix + REGULARIZE * jnp.eye(4, dtype=gram_matrix.dtype)
    right_side = cross_matrix + REGULARIZE * old_pose
    factor = jnp.linalg.cholesky(left_side)
    solved = jax.scipy.linalg.cho_solve((factor, True), right_side.T)
    new_pose = solved.T
    return jnp.concatenate([new_pose[:, :3].reshape(9), new_pose[:, 3]])

def reference(points, rows, cells, pose):
    margin = NCELL * CT
    live_slots = rows >= 0
    safe_rows = jnp.where(live_slots, rows, 0)

    def pick(segment_points, segment_rows):
        taken = jnp.take(segment_points, segment_rows.reshape(-1), axis=1)
        return taken.reshape(3, 2, SLOTS).transpose(1, 0, 2)
    raw_source = jax.vmap(jax.vmap(pick))(points, safe_rows)
    ones_row = jnp.ones(raw_source.shape[:3] + (1,) + raw_source.shape[4:], raw_source.dtype)
    extended = jnp.concatenate([raw_source, ones_row], axis=3)
    spread = jnp.float32(SPREAD_START)
    pose_now = pose
    result = None
    for iteration in range(ITERS):
        linear_part = pose_now[:9].T.reshape(LINES, 3, 3)
        offset_part = pose_now[9:].T
        world_points = jnp.einsum('lkm,lgmn->lgkn', linear_part, points, precision=lax.Precision.HIGHEST) + offset_part[:, None, :, None]
        moved_source = jnp.einsum('lkm,lgdms->lgdks', linear_part, raw_source, precision=lax.Precision.HIGHEST) + offset_part[:, None, None, :, None]

        def device(index):
            line_pos = index // SEGS
            seg_pos = index % SEGS
            lower_line = jnp.maximum(line_pos - 1, 0)
            upper_line = jnp.minimum(line_pos + 1, LINES - 1)
            targets = jnp.stack([world_points[lower_line, seg_pos][:, NPTS - margin:], world_points[upper_line, seg_pos][:, :margin]])
            blocks = moved_source[line_pos, seg_pos].reshape(2, 3, NBLK, BLOCK).transpose(0, 2, 1, 3)
            block_cells = cells[line_pos, seg_pos]

            def direction(target_world, direction_blocks, direction_cells):
                return jax.vmap(lambda block_points, block_cell: match_block(block_points, block_cell, target_world, spread))(direction_blocks, direction_cells)
            output = jax.vmap(direction)(targets, blocks, block_cells)
            return output.transpose(0, 2, 1, 3).reshape(2, 5, SLOTS)
        result = lax.map(device, jnp.arange(LINES * SEGS, dtype=jnp.int32)).reshape(LINES, SEGS, 2, 5, SLOTS)
        result = result * live_slots[:, :, :, None, :].astype(result.dtype)
        pulled = result[:, :, :, :3]
        share_all = result[:, :, :, 3]
        energy_all = result[:, :, :, 4]
        gram_lines = jnp.einsum('lgdks,lgdms->lkm', extended * share_all[:, :, :, None, :], extended, precision=lax.Precision.HIGHEST)
        cross_lines = jnp.einsum('lgdks,lgdms->lkm', pulled, extended, precision=lax.Precision.HIGHEST)
        pose_now = jax.vmap(solve_pose)(gram_lines, cross_lines, pose_now.T).T
        spread = (jnp.sum(energy_all) + PRIOR_TOP) / (3.0 * jnp.sum(share_all) + PRIOR_BOTTOM)
    return (result, pose_now, spread.reshape(1))
```

```python
import functools
import math

import jax
import jax.numpy as jnp
from jax import lax
from jax.experimental import pallas as pl
from jax.experimental.pallas import tpu as pltpu
from jax.sharding import PartitionSpec as P

NCELL = 16
CT = 512
BLOCK = 128
ITERS = 2
SPREAD_START = 0.05
PRIOR_TOP = 0.05
LOG2E = math.log2(math.e)
MARGIN = NCELL * CT
CHUNK = 16
MESH = pl.DeviceIdType.MESH
F32 = jnp.float32


def iota(shape, dim):
    return lax.broadcasted_iota(jnp.int32, shape, dim)


def fetch_kernel(lines, segs, points, rows, pose, near, near_pose, src, own, table, own_sem, send_sem, recv_sem):
    me = lax.axis_index("line")
    upper, lower = lax.rem(me + 1, lines), lax.rem(me + lines - 1, lines)
    npts = points.shape[1]
    low_cols = pl.ds(0, MARGIN)
    high_cols = pl.ds(npts - MARGIN, MARGIN)

    barrier = pltpu.get_barrier_semaphore()
    for peer in (lower, upper):
        pl.semaphore_signal(barrier, inc=1, device_id={"line": peer}, device_id_type=MESH)
    locals_ = [
        pltpu.make_async_copy(points.at[:, cols], own.at[d], own_sem.at[d])
        for d, cols in enumerate((low_cols, high_cols))
    ]
    for copy in locals_:
        copy.start()
    pl.semaphore_wait(barrier, 2)

    def remote(source, target, slot, peer):
        return pltpu.make_async_remote_copy(
            src_ref=source,
            dst_ref=target,
            send_sem=send_sem.at[slot],
            recv_sem=recv_sem.at[slot],
            device_id={"line": peer},
            device_id_type=MESH,
        )

    sends = [
        remote(points.at[:, high_cols], near.at[0], 0, upper),
        remote(points.at[:, low_cols], near.at[1], 1, lower),
        remote(pose, near_pose.at[0], 2, upper),
        remote(pose, near_pose.at[1], 3, lower),
    ]
    for copy in sends:
        copy.start()

    table[...] = jnp.zeros_like(table)
    for copy in locals_:
        copy.wait()
    pairs = MARGIN // 256
    for d in range(2):
        for u in range(pairs):
            table[d, u, 0:3, :] = own[d, :, 256 * u : 256 * u + 128]
            table[d, u, 4:7, :] = own[d, :, 256 * u + 128 : 256 * u + 256]

    sub = iota((8, BLOCK), 0)
    shift = (sub >= 4).astype(jnp.int32)
    blocks = rows.shape[1] // BLOCK
    for d in range(2):

        @pl.loop(0, blocks)
        def _(b):
            index = rows[d : d + 1, pl.ds(pl.multiple_of(b * BLOCK, BLOCK), BLOCK)]
            live = index >= 0
            local = index if d == 0 else index - (npts - MARGIN)
            lane = jnp.broadcast_to(jnp.bitwise_and(local, 127), (8, BLOCK))
            high = jnp.broadcast_to(jnp.right_shift(local, 7), (8, BLOCK)) - shift
            total = jnp.zeros((8, BLOCK), F32)
            for u in range(pairs):
                taken = jnp.take_along_axis(table[d, u], lane, axis=1, mode="promise_in_bounds")
                total = jnp.where(high == 2 * u, taken, total)
            both = total + pltpu.roll(total, 4, 0)
            alive = jnp.broadcast_to(live.astype(F32), (8, BLOCK))
            tail = jnp.where(sub == 3, 1.0, jnp.where(sub == 4, alive, 0.0))
            src[d * blocks + b] = jnp.where(sub < 3, both, tail)

    for copy in sends:
        copy.wait()


def fetch(points, rows, pose, lines, segs):
    blocks = rows.shape[0] * rows.shape[1] // BLOCK
    vmem = pl.BlockSpec(memory_space=pltpu.VMEM)
    return pl.pallas_call(
        functools.partial(fetch_kernel, lines, segs),
        out_shape=(
            jax.ShapeDtypeStruct((2, 3, MARGIN), F32),
            jax.ShapeDtypeStruct((2, 12, 1), F32),
            jax.ShapeDtypeStruct((blocks, 8, BLOCK), F32),
        ),
        in_specs=[pl.BlockSpec(memory_space=pl.ANY), vmem, vmem],
        out_specs=(vmem, vmem, vmem),
        scratch_shapes=[
            pltpu.VMEM((2, 3, MARGIN), F32),
            pltpu.VMEM((2, MARGIN // 256, 8, 128), F32),
            pltpu.SemaphoreType.DMA((2,)),
            pltpu.SemaphoreType.DMA((4,)),
            pltpu.SemaphoreType.DMA((4,)),
        ],
        compiler_params=pltpu.CompilerParams(collective_id=0, has_side_effects=True),
        name="fetch",
    )(points, rows, pose)


def pose_columns(column):
    wide = jnp.broadcast_to(column, (12, BLOCK))
    sub = iota((8, BLOCK), 0)
    zero = jnp.zeros((8, BLOCK), F32)
    columns = []
    for c in range(4):
        value = jnp.where(sub == 3, 1.0, zero) if c == 3 else zero
        for k in range(3):
            row = 3 * k + c if c < 3 else 9 + k
            value = jnp.where(sub == k, jnp.broadcast_to(wide[row : row + 1], (8, BLOCK)), value)
        columns.append(value)
    return columns


def apply_pose(columns, tile):
    total = columns[3]
    for c in range(3):
        total = total + columns[c] * jnp.broadcast_to(tile[c : c + 1], (8, BLOCK))
    return total


def em_kernel(
    lines, segs, src, near, near_pose, pose, cells, matched, fitted, final_spread,
    targets, halves, weights, energies, row_out, line_out, seg_in, line_in,
    seg_send, seg_recv, line_send, line_recv,
):
    my_line, my_seg = lax.axis_index("line"), lax.axis_index("seg")
    blocks = src.shape[0] // 2
    tiles = CT // BLOCK
    sub = iota((8, BLOCK), 0)
    lanes = iota((8, BLOCK), 1)

    barrier = pltpu.get_barrier_semaphore()

    @pl.loop(1, segs)
    def _(k):
        pl.semaphore_signal(
            barrier, inc=1, device_id={"seg": lax.rem(my_seg + k, segs)}, device_id_type=MESH
        )

    @pl.loop(1, lines)
    def _(k):
        pl.semaphore_signal(
            barrier, inc=1, device_id={"line": lax.rem(my_line + k, lines)}, device_id_type=MESH
        )

    def seg_copy(it, k):
        return pltpu.make_async_remote_copy(
            src_ref=row_out.at[it],
            dst_ref=seg_in.at[it, my_seg],
            send_sem=seg_send.at[it, k],
            recv_sem=seg_recv.at[it, my_seg],
            device_id={"seg": lax.rem(my_seg + k, segs)},
            device_id_type=MESH,
        )

    def line_copy(it, k):
        return pltpu.make_async_remote_copy(
            src_ref=line_out.at[it],
            dst_ref=line_in.at[it, my_line],
            send_sem=line_send.at[it, k],
            recv_sem=line_recv.at[it, my_line],
            device_id={"line": lax.rem(my_line + k, lines)},
            device_id_type=MESH,
        )

    def seg_arrival(it, k):
        other = lax.rem(my_seg + k, segs)
        return pltpu.make_async_remote_copy(
            src_ref=row_out.at[it],
            dst_ref=seg_in.at[it, other],
            send_sem=seg_send.at[it, k],
            recv_sem=seg_recv.at[it, other],
            device_id={"seg": other},
            device_id_type=MESH,
        )

    def line_arrival(it, k):
        other = lax.rem(my_line + k, lines)
        return pltpu.make_async_remote_copy(
            src_ref=line_out.at[it],
            dst_ref=line_in.at[it, other],
            send_sem=line_send.at[it, k],
            recv_sem=line_recv.at[it, other],
            device_id={"line": other},
            device_id_type=MESH,
        )

    own_pose = pose_columns(pose[...])
    low_pose = pose_columns(near_pose[0])
    up_pose = pose_columns(near_pose[1])
    spread = jnp.full((8, BLOCK), SPREAD_START, F32)

    for it in range(ITERS):
        last = it == ITERS - 1
        square = LOG2E / (2.0 * spread)
        scale = jnp.sqrt(square)
        back = 1.0 / scale
        back_square = 2.0 * spread / LOG2E
        rows_scale = jnp.where(sub < 3, scale, 1.0)
        own_scaled = [column * rows_scale for column in own_pose]
        near_scaled = [
            [column * rows_scale for column in low_pose],
            [column * rows_scale for column in up_pose],
        ]
        row_back = jnp.where(sub < 3, back, jnp.where(sub == 4, back_square, 1.0))

        for d in range(2):

            @pl.loop(0, NCELL)
            def _(c):
                for t in range(tiles):
                    start = pl.multiple_of(c * CT + t * BLOCK, BLOCK)
                    tile = near[d, :, pl.ds(start, BLOCK)]
                    value = apply_pose(near_scaled[d], tile)
                    here = slice(t * BLOCK, (t + 1) * BLOCK)
                    targets[d * NCELL + c, :, here] = value
                    first = value.astype(jnp.bfloat16).astype(F32)
                    rest = value - first
                    second = rest.astype(jnp.bfloat16).astype(F32)
                    third = rest - second
                    packed = jnp.concatenate([first, second, third, jnp.zeros_like(first)], axis=0)
                    halves[d * NCELL + c, :, here] = packed.astype(jnp.bfloat16)

        sums = [jnp.zeros((8, BLOCK), F32) for _ in range(7)]
        for d in range(2):

            def one_block(b, sums):
                x = src[d * blocks + b]
                cell = jnp.maximum(cells[d, b], 0) + d * NCELL
                moved = jnp.transpose(apply_pose(own_scaled, x))
                y = [targets[cell, k : k + 1, :] for k in range(3)]
                for i in range(BLOCK // CHUNK):
                    here = slice(i * CHUNK, (i + 1) * CHUNK)
                    distance = None
                    for k in range(3):
                        gap = moved[here, k : k + 1] - y[k]
                        distance = gap * gap if distance is None else distance + gap * gap
                    weight = lax.exp2(-distance)
                    part = weight * distance
                    energy = part[:, :BLOCK]
                    for t in range(1, tiles):
                        energy = energy + part[:, t * BLOCK : (t + 1) * BLOCK]
                    energies[here, :] = energy
                    high = weight.astype(jnp.bfloat16)
                    weights[here, :] = high
                    weights[BLOCK + i * CHUNK : BLOCK + (i + 1) * CHUNK, :] = (
                        weight - high.astype(F32)
                    ).astype(jnp.bfloat16)
                out = lax.dot_general(
                    halves[cell],
                    weights[...],
                    (((1,), (1,)), ((), ())),
                    preferred_element_type=F32,
                )
                out = out[:, :BLOCK] + out[:, BLOCK:]
                pulled = out[0:8] + (out[8:16] + jnp.where(sub == 3, 0.0, out[16:24]))
                energy = jnp.sum(jnp.transpose(energies[...]), axis=0, keepdims=True)
                total = pulled[3:4]
                factor = x[4:5] / (total + 1.0)
                merged = jnp.where(sub == 4, jnp.broadcast_to(energy, (8, BLOCK)), pulled)
                result = merged * row_back * jnp.broadcast_to(factor, (8, BLOCK))
                if last:
                    matched[d, :, pl.ds(pl.multiple_of(b * BLOCK, BLOCK), BLOCK)] = result[0:5]
                share = jnp.broadcast_to(result[3:4], (8, BLOCK))
                weighted = share * x
                new = []
                for c in range(4):
                    new.append(sums[c] + (result * jnp.broadcast_to(x[c : c + 1], (8, BLOCK)) if c < 3 else result))
                for c in range(3):
                    new.append(sums[4 + c] + weighted * jnp.broadcast_to(x[c : c + 1], (8, BLOCK)))
                return tuple(new)

            sums = lax.fori_loop(0, blocks, one_block, tuple(sums))

        row = jnp.zeros((8, BLOCK), F32)
        for q in range(7):
            column = jnp.sum(sums[q], axis=1, keepdims=True)
            row = row + jnp.where(lanes == 8 * q + sub, jnp.broadcast_to(column, (8, BLOCK)), 0.0)
        row = jnp.sum(row, axis=0, keepdims=True)
        row_out[it] = row
        seg_in[it, my_seg] = row
        if it == 0:
            pl.semaphore_wait(barrier, segs + lines - 2)

        @pl.loop(1, segs)
        def _(k):
            seg_copy(it, k).start()

        kept = jnp.zeros((8, BLOCK), F32)
        for c in range(4):
            kept = kept + jnp.where((lanes == 64 + 8 * c + sub) & (sub < 3), own_pose[c], 0.0)
        kept = jnp.sum(kept, axis=0, keepdims=True)

        @pl.loop(1, segs)
        def _(k):
            seg_arrival(it, k).wait_recv()

        line_row = kept + jnp.sum(seg_in[it], axis=0)
        line_out[it] = line_row
        line_in[it, my_line] = line_row

        @pl.loop(1, lines)
        def _(k):
            line_copy(it, k).start()

        @pl.loop(1, lines)
        def _(k):
            line_arrival(it, k).wait_recv()

        whole = line_in[it].reshape(lines, BLOCK)
        turned = jnp.transpose(jnp.concatenate([whole, jnp.zeros((BLOCK - lines, BLOCK), F32)], axis=0))
        part = [turned[8 * q : 8 * q + 8] for q in range(12)]

        def entry(q, r):
            return jnp.broadcast_to(part[q][r : r + 1], (8, BLOCK))

        n = [[None] * 4 for _ in range(4)]
        for a in range(3):
            for c in range(a + 1):
                n[a][c] = entry(4 + c, a)
        for c in range(4):
            n[3][c] = entry(c, 3)
        share_sum = jnp.sum(n[3][3], axis=1, keepdims=True)
        energy_sum = jnp.sum(entry(3, 4), axis=1, keepdims=True)
        spread = jnp.broadcast_to((energy_sum + PRIOR_TOP) / (3.0 * share_sum + 1.0), (8, BLOCK))
        for a in range(4):
            n[a][a] = n[a][a] + 1.0
        low = [[None] * 4 for _ in range(4)]
        inverse = [None] * 4
        for c in range(4):
            diagonal = n[c][c]
            for j in range(c):
                diagonal = diagonal - low[c][j] * n[c][j]
            inverse[c] = 1.0 / diagonal
            for a in range(c + 1, 4):
                for j in range(c):
                    n[a][c] = n[a][c] - low[c][j] * n[a][j]
                low[a][c] = n[a][c] * inverse[c]
        z = [part[c] + part[8 + c] for c in range(4)]
        for a in range(4):
            for c in range(a):
                z[a] = z[a] - low[a][c] * z[c]
        z = [z[a] * inverse[a] for a in range(4)]
        for a in range(3, -1, -1):
            for c in range(a + 1, 4):
                z[a] = z[a] - low[c][a] * z[c]

        def pick(which):
            columns = []
            for c in range(4):
                value = jnp.sum(jnp.where((lanes == which) & (sub < 3), z[c], 0.0), axis=1, keepdims=True)
                value = jnp.broadcast_to(value, (8, BLOCK))
                columns.append(jnp.where(sub == 3, 1.0, value) if c == 3 else value)
            return columns

        own_pose = pick(my_line)
        if not last:
            low_pose = pick(my_line - 1)
            up_pose = pick(my_line + 1)

    for k in range(3):
        for c in range(3):
            fitted[3 * k + c : 3 * k + c + 1, :] = own_pose[c][k : k + 1, 0:1]
        fitted[9 + k : 10 + k, :] = own_pose[3][k : k + 1, 0:1]
    final_spread[...] = spread[0:1, 0:1]

    for it in range(ITERS):

        @pl.loop(1, segs)
        def _(k):
            seg_copy(it, k).wait_send()

        @pl.loop(1, lines)
        def _(k):
            line_copy(it, k).wait_send()


def em(src, near, near_pose, pose, cells, lines, segs):
    blocks = src.shape[0]
    vmem = pl.BlockSpec(memory_space=pltpu.VMEM)
    smem = pl.BlockSpec(memory_space=pltpu.SMEM)
    return pl.pallas_call(
        functools.partial(em_kernel, lines, segs),
        out_shape=(
            jax.ShapeDtypeStruct((2, 5, blocks // 2 * BLOCK), F32),
            jax.ShapeDtypeStruct((12, 1), F32),
            jax.ShapeDtypeStruct((1, 1), F32),
        ),
        in_specs=[vmem, vmem, vmem, vmem, smem],
        out_specs=(vmem, vmem, vmem),
        scratch_shapes=[
            pltpu.VMEM((2 * NCELL, 8, CT), F32),
            pltpu.VMEM((2 * NCELL, 32, CT), jnp.bfloat16),
            pltpu.VMEM((2 * BLOCK, CT), jnp.bfloat16),
            pltpu.VMEM((BLOCK, BLOCK), F32),
            pltpu.VMEM((ITERS, 1, BLOCK), F32),
            pltpu.VMEM((ITERS, 1, BLOCK), F32),
            pltpu.VMEM((ITERS, segs, 1, BLOCK), F32),
            pltpu.VMEM((ITERS, lines, 1, BLOCK), F32),
            pltpu.SemaphoreType.DMA((ITERS, segs)),
            pltpu.SemaphoreType.DMA((ITERS, segs)),
            pltpu.SemaphoreType.DMA((ITERS, lines)),
            pltpu.SemaphoreType.DMA((ITERS, lines)),
        ],
        compiler_params=pltpu.CompilerParams(collective_id=1, has_side_effects=True),
        name="em",
    )(src, near, near_pose, pose, cells)


def solution(mesh):
    lines, segs = mesh.shape["line"], mesh.shape["seg"]

    def on_device(points, rows, cells, pose):
        near, near_pose, src = fetch(points[0, 0], rows[0, 0], pose, lines, segs)
        matched, fitted, spread = em(src, near, near_pose, pose, cells[0, 0], lines, segs)
        return matched[None, None], fitted, spread.reshape(1)

    return jax.shard_map(
        on_device,
        mesh=mesh,
        in_specs=(
            P("line", "seg", None, None),
            P("line", "seg", None, None),
            P("line", "seg", None, None),
            P(None, "line"),
        ),
        out_specs=(P("line", "seg", None, None, None), P(None, "line"), P()),
        check_vma=False,
    )
```

```python
import functools
import math

import jax
import jax.numpy as jnp
from jax import lax
from jax.experimental import pallas as pl
from jax.experimental.pallas import tpu as pltpu
from jax.sharding import PartitionSpec as P

NCELL = 16
CT = 512
BLOCK = 128
ITERS = 2
SPREAD_START = 0.05
PRIOR_TOP = 0.05
LOG2E = math.log2(math.e)
MARGIN = NCELL * CT
CHUNK = 16
UNROLL = 8
GATHER = 4
VMEM_LIMIT = 16 << 20
MESH = pl.DeviceIdType.MESH
F32 = jnp.float32


def iota(shape, dim):
    return lax.broadcasted_iota(jnp.int32, shape, dim)


def fetch_kernel(lines, points, rows, pose, near, near_pose, src, own, own_sem, send_sem, recv_sem):
    me = lax.axis_index("line")
    upper, lower = lax.rem(me + 1, lines), lax.rem(me + lines - 1, lines)
    tiles = points.shape[1]
    margin_tiles = MARGIN // BLOCK
    low_tiles = pl.ds(0, margin_tiles)
    high_tiles = pl.ds(tiles - margin_tiles, margin_tiles)

    barrier = pltpu.get_barrier_semaphore()
    for peer in (lower, upper):
        pl.semaphore_signal(barrier, inc=1, device_id={"line": peer}, device_id_type=MESH)
    locals_ = [
        pltpu.make_async_copy(points.at[:, part], own.at[d], own_sem.at[d])
        for d, part in enumerate((low_tiles, high_tiles))
    ]
    for copy in locals_:
        copy.start()

    def remote(source, target, slot, peer):
        return pltpu.make_async_remote_copy(
            src_ref=source,
            dst_ref=target,
            send_sem=send_sem.at[slot],
            recv_sem=recv_sem.at[slot],
            device_id={"line": peer},
            device_id_type=MESH,
        )

    sends = [
        remote(points.at[:, high_tiles], near.at[0], 0, upper),
        remote(points.at[:, low_tiles], near.at[1], 1, lower),
        remote(pose, near_pose.at[0], 2, upper),
        remote(pose, near_pose.at[1], 3, lower),
    ]
    sub = iota((8, BLOCK), 0)
    blocks = rows.shape[1] // BLOCK

    def gather(d):
        @pl.loop(0, blocks // GATHER)
        def _(turn):
            for g in range(GATHER):
                b = turn * GATHER + g
                index = rows[d : d + 1, pl.ds(pl.multiple_of(b * BLOCK, BLOCK), BLOCK)]
                live = index >= 0
                local = index if d == 0 else index - (tiles * BLOCK - MARGIN)
                lane = jnp.broadcast_to(jnp.bitwise_and(local, 127), (8, BLOCK))
                high = jnp.broadcast_to(jnp.right_shift(local, 7), (8, BLOCK)) - sub
                found = [jnp.zeros((8, BLOCK), F32) for _ in range(3)]
                for u in range(margin_tiles // 8):
                    here = high == 8 * u
                    for k in range(3):
                        taken = jnp.take_along_axis(
                            own[d, k, 8 * u : 8 * u + 8, :], lane, axis=1, mode="promise_in_bounds"
                        )
                        found[k] = jnp.where(here, taken, found[k])
                alive = jnp.broadcast_to(live.astype(F32), (8, BLOCK))
                value = jnp.where(sub == 3, 1.0, jnp.where(sub == 4, alive, 0.0))
                for k in range(3):
                    picked = jnp.sum(found[k], axis=0, keepdims=True)
                    value = jnp.where(sub == k, jnp.broadcast_to(picked, (8, BLOCK)), value)
                src[d * blocks + b] = value

    pl.semaphore_wait(barrier, 2)
    for copy in sends:
        copy.start()
    for d in range(2):
        locals_[d].wait()
        gather(d)
    for copy in sends:
        copy.wait()


def fetch(points, rows, pose, lines):
    blocks = rows.shape[0] * rows.shape[1] // BLOCK
    vmem = pl.BlockSpec(memory_space=pltpu.VMEM)
    return pl.pallas_call(
        functools.partial(fetch_kernel, lines),
        out_shape=(
            jax.ShapeDtypeStruct((2, 3, MARGIN // BLOCK, BLOCK), F32),
            jax.ShapeDtypeStruct((2, 1, 12), F32),
            jax.ShapeDtypeStruct((blocks, 8, BLOCK), F32),
        ),
        in_specs=[pl.BlockSpec(memory_space=pl.ANY), vmem, vmem],
        out_specs=(vmem, vmem, vmem),
        scratch_shapes=[
            pltpu.VMEM((2, 3, MARGIN // BLOCK, BLOCK), F32),
            pltpu.SemaphoreType.DMA((2,)),
            pltpu.SemaphoreType.DMA((4,)),
            pltpu.SemaphoreType.DMA((4,)),
        ],
        compiler_params=pltpu.CompilerParams(
            collective_id=0, has_side_effects=True, vmem_limit_bytes=VMEM_LIMIT
        ),
        name="fetch",
    )(points, rows, pose)


def pose_columns(row):
    sub = iota((8, BLOCK), 0)
    columns = []
    for c in range(4):
        value = jnp.zeros((8, BLOCK), F32)
        for k in range(3):
            lane = 3 * k + c if c < 3 else 9 + k
            value = jnp.where(sub == k, jnp.broadcast_to(row[:, lane : lane + 1], (8, BLOCK)), value)
        columns.append(value)
    return columns


def apply_pose(columns, coordinates):
    total = columns[3]
    for c in range(3):
        total = total + columns[c] * jnp.broadcast_to(coordinates[c], (8, BLOCK))
    return total


def split3(value):
    first = value.astype(jnp.bfloat16).astype(F32)
    rest = value - first
    second = rest.astype(jnp.bfloat16).astype(F32)
    return first, second, rest - second


def operand(value, norm_first):
    sub = iota((8, BLOCK), 0)
    norm = -jnp.sum(value * value, axis=0, keepdims=True)
    norms = [jnp.broadcast_to(part, (8, BLOCK)) for part in split3(norm)]
    if norm_first:
        value = 2.0 * value
        order = (0, 0, 0, 1, 1, 2, 1, 2)
        extra = norms + [1.0, 1.0, 1.0]
    else:
        order = (0, 1, 2, 0, 1, 0, 2, 1)
        extra = [1.0, 1.0, 1.0] + norms
    parts = split3(value)
    groups = [parts[p] for p in order]
    for i in range(6):
        groups[i] = jnp.where(sub == 3, extra[i], groups[i])
    return jnp.concatenate(groups, axis=0)


def em_kernel(
    lines, segs, src, near, near_pose, pose, cells, matched, fitted, final_spread,
    side_y, side_m, centres, weights, energies, row_out, line_out, seg_in, line_in,
    seg_send, seg_recv, line_send, near_recv, line_recv,
):
    my_line, my_seg = lax.axis_index("line"), lax.axis_index("seg")
    blocks = src.shape[0] // 2
    tiles = CT // BLOCK
    sub = iota((8, BLOCK), 0)
    lanes = iota((8, BLOCK), 1)

    barrier = pltpu.get_barrier_semaphore()

    @pl.loop(1, segs)
    def _(k):
        pl.semaphore_signal(
            barrier, inc=1, device_id={"seg": lax.rem(my_seg + k, segs)}, device_id_type=MESH
        )

    @pl.loop(1, lines)
    def _(k):
        pl.semaphore_signal(
            barrier, inc=1, device_id={"line": lax.rem(my_line + k, lines)}, device_id_type=MESH
        )

    seg_order = sorted(range(1, segs), key=lambda k: -min(k, segs - k))
    line_order = [1, lines - 1] + sorted(range(2, lines - 1), key=lambda k: -min(k, lines - k))

    def seg_copy(it, k):
        return pltpu.make_async_remote_copy(
            src_ref=row_out.at[it],
            dst_ref=seg_in.at[it, my_seg],
            send_sem=seg_send.at[it],
            recv_sem=seg_recv.at[it],
            device_id={"seg": lax.rem(my_seg + k, segs)},
            device_id_type=MESH,
        )

    def line_copy(it, k):
        arrived = line_recv.at[it]
        if k == 1:
            arrived = near_recv.at[it, 0]
        elif k == lines - 1:
            arrived = near_recv.at[it, 1]
        return pltpu.make_async_remote_copy(
            src_ref=line_out.at[it],
            dst_ref=line_in.at[it, my_line],
            send_sem=line_send.at[it],
            recv_sem=arrived,
            device_id={"line": lax.rem(my_line + k, lines)},
            device_id_type=MESH,
        )

    def wait_rows(buffer, count, sem):
        part = buffer.at[pl.ds(0, count)]
        pltpu.make_async_copy(part, part, sem).wait()

    lower, upper = lax.rem(my_line + lines - 1, lines), lax.rem(my_line + 1, lines)

    own_pose = pose_columns(pose[...])
    low_pose = pose_columns(near_pose[0])
    up_pose = pose_columns(near_pose[1])
    spread = jnp.full((8, BLOCK), SPREAD_START, F32)

    def prepare(own_pose, low_pose, up_pose):
        for d in range(2):

            @pl.loop(0, NCELL)
            def _(c):
                world = []
                for t in range(tiles):
                    raw = [near[d, k, pl.ds(c * tiles + t, 1), :] for k in range(3)]
                    world.append(apply_pose((low_pose, up_pose)[d], raw))
                centre = world[0]
                for t in range(1, tiles):
                    centre = centre + world[t]
                centre = jnp.sum(centre, axis=1, keepdims=True) * (1.0 / CT)
                centre = jnp.broadcast_to(centre, (8, BLOCK))
                centres[d * NCELL + c] = centre
                for t in range(tiles):
                    here = slice(t * BLOCK, (t + 1) * BLOCK)
                    value = operand(world[t] - centre, False)
                    side_y[d * NCELL + c, :, here] = value.astype(jnp.bfloat16)

        for d in range(2):

            @pl.loop(0, blocks // UNROLL)
            def _(turn):
                for u in range(UNROLL):
                    b = turn * UNROLL + u
                    x = src[d * blocks + b]
                    cell = jnp.maximum(cells[d, b], 0) + d * NCELL
                    moved = apply_pose(own_pose, [x[k : k + 1] for k in range(3)])
                    value = operand(moved - centres[cell], True)
                    side_m[d * blocks + b] = jnp.transpose(value).astype(jnp.bfloat16)

    prepare(own_pose, low_pose, up_pose)
    for it in range(ITERS):
        last = it == ITERS - 1
        rate = LOG2E / (2.0 * spread)
        rate = jnp.concatenate([rate] * (CHUNK // 8), axis=0)
        rate = jnp.concatenate([rate] * tiles, axis=1)

        sums = [jnp.zeros((8, BLOCK), F32) for _ in range(7)]
        for d in range(2):

            def one_block(b, u, sums):
                x = src[d * blocks + b]
                cell = jnp.maximum(cells[d, b], 0) + d * NCELL
                exponents = jnp.dot(side_m[d * blocks + b], side_y[cell], preferred_element_type=F32)
                for i in range(BLOCK // CHUNK):
                    here = slice(i * CHUNK, (i + 1) * CHUNK)
                    exponent = exponents[here]
                    weight = lax.exp2(exponent * rate)
                    part = weight * exponent
                    energy = part[:, :BLOCK]
                    for t in range(1, tiles):
                        energy = energy + part[:, t * BLOCK : (t + 1) * BLOCK]
                    energies[u, here, :] = energy
                    high = weight.astype(jnp.bfloat16)
                    weights[u, here, 0:CT] = high
                    weights[u, here, CT : 2 * CT] = (weight - high.astype(F32)).astype(jnp.bfloat16)
                values = side_y[cell, 0:32, :]
                out = lax.dot_general(
                    weights[u],
                    jnp.concatenate([values, values], axis=1),
                    (((1,), (1,)), ((), ())),
                    preferred_element_type=F32,
                )
                out = jnp.transpose(out)
                pulled = out[0:8] + jnp.where(sub == 3, 0.0, out[8:16] + out[16:24])
                energy = jnp.sum(jnp.transpose(energies[u]), axis=0, keepdims=True)
                total = jnp.broadcast_to(pulled[3:4], (8, BLOCK))
                factor = jnp.broadcast_to(x[4:5], (8, BLOCK)) / (total + 1.0)
                merged = jnp.where(sub == 4, jnp.broadcast_to(-energy, (8, BLOCK)), pulled)
                result = (merged + centres[cell] * total) * factor
                if last:
                    here = pl.ds(pl.multiple_of(b * BLOCK, BLOCK), BLOCK)
                    for k in range(5):
                        matched[k, d : d + 1, here] = result[k : k + 1]
                share = jnp.broadcast_to(result[3:4], (8, BLOCK))
                weighted = share * x
                new = []
                for c in range(4):
                    new.append(sums[c] + (result * jnp.broadcast_to(x[c : c + 1], (8, BLOCK)) if c < 3 else result))
                for c in range(3):
                    new.append(sums[4 + c] + weighted * jnp.broadcast_to(x[c : c + 1], (8, BLOCK)))
                return tuple(new)

            def some_blocks(turn, sums):
                for u in range(UNROLL):
                    sums = one_block(turn * UNROLL + u, u, sums)
                return sums

            sums = lax.fori_loop(0, blocks // UNROLL, some_blocks, tuple(sums))

        row = jnp.zeros((8, BLOCK), F32)
        for q in range(7):
            column = jnp.sum(sums[q], axis=1, keepdims=True)
            row = row + jnp.where(lanes == 8 * q + sub, jnp.broadcast_to(column, (8, BLOCK)), 0.0)
        row = jnp.sum(row, axis=0, keepdims=True)
        row_out[it] = row
        seg_in[it, my_seg] = row
        if it == 0:
            pl.semaphore_wait(barrier, segs + lines - 2)
        for k in seg_order:
            seg_copy(it, k).start()

        kept = jnp.zeros((8, BLOCK), F32)
        for c in range(4):
            kept = kept + jnp.where((lanes == 64 + 8 * c + sub) & (sub < 3), own_pose[c], 0.0)
        kept = jnp.sum(kept, axis=0, keepdims=True)

        wait_rows(seg_in.at[it], segs - 1, seg_recv.at[it])
        line_row = kept + jnp.sum(seg_in[it], axis=0)
        line_out[it] = line_row
        line_in[it, my_line] = line_row
        for k in line_order:
            line_copy(it, k).start()
        wait_rows(seg_in.at[it], segs - 1, seg_send.at[it])
        for k in range(2):
            wait_rows(line_in.at[it], 1, near_recv.at[it, k])

        three = jnp.where(sub == 0, line_in[it, lower], jnp.where(sub == 1, line_row, line_in[it, upper]))
        turned = jnp.transpose(three)
        part = [jnp.concatenate([turned[8 * q : 8 * q + 8], jnp.zeros((8, BLOCK - 8), F32)], axis=1) for q in range(12)]

        def entry(q, r):
            return jnp.broadcast_to(part[q][r : r + 1], (8, BLOCK))

        n = [[None] * 4 for _ in range(4)]
        for a in range(3):
            for c in range(a + 1):
                n[a][c] = entry(4 + c, a)
        for c in range(4):
            n[3][c] = entry(c, 3)
        for a in range(4):
            n[a][a] = n[a][a] + 1.0
        low = [[None] * 4 for _ in range(4)]
        inverse = [None] * 4
        for c in range(4):
            diagonal = n[c][c]
            for j in range(c):
                diagonal = diagonal - low[c][j] * n[c][j]
            inverse[c] = 1.0 / diagonal
            for a in range(c + 1, 4):
                for j in range(c):
                    n[a][c] = n[a][c] - low[c][j] * n[a][j]
                low[a][c] = n[a][c] * inverse[c]
        z = [part[c] + part[8 + c] for c in range(4)]
        for a in range(4):
            for c in range(a):
                z[a] = z[a] - low[a][c] * z[c]
        z = [z[a] * inverse[a] for a in range(4)]
        for a in range(3, -1, -1):
            for c in range(a + 1, 4):
                z[a] = z[a] - low[c][a] * z[c]

        def pick(which):
            columns = []
            for c in range(4):
                value = jnp.sum(jnp.where((lanes == which) & (sub < 3), z[c], 0.0), axis=1, keepdims=True)
                columns.append(jnp.broadcast_to(value, (8, BLOCK)))
            return columns

        own_pose = pick(1)
        if not last:
            low_pose, up_pose = pick(0), pick(2)
            prepare(own_pose, low_pose, up_pose)
        wait_rows(line_in.at[it], lines - 3, line_recv.at[it])
        totals = jnp.sum(line_in[it], axis=0)
        spread = (totals[:, 28:29] + PRIOR_TOP) / (3.0 * totals[:, 27:28] + 1.0)
        spread = jnp.broadcast_to(spread, (8, BLOCK))
        wait_rows(line_in.at[it], lines - 1, line_send.at[it])

    line = jnp.zeros((8, BLOCK), F32)
    for c in range(4):
        lane = 3 * sub + c if c < 3 else 9 + sub
        line = line + jnp.where((lanes == lane) & (sub < 3), own_pose[c], 0.0)
    fitted[...] = jnp.sum(line, axis=0, keepdims=True)[:, 0:12]
    final_spread[...] = spread[0:1, 0:1]


def em(src, near, near_pose, pose, cells, lines, segs):
    blocks = src.shape[0]
    vmem = pl.BlockSpec(memory_space=pltpu.VMEM)
    smem = pl.BlockSpec(memory_space=pltpu.SMEM)
    return pl.pallas_call(
        functools.partial(em_kernel, lines, segs),
        out_shape=(
            jax.ShapeDtypeStruct((5, 2, blocks // 2 * BLOCK), F32),
            jax.ShapeDtypeStruct((1, 12), F32),
            jax.ShapeDtypeStruct((1, 1), F32),
        ),
        in_specs=[vmem, vmem, vmem, vmem, smem],
        out_specs=(vmem, vmem, vmem),
        scratch_shapes=[
            pltpu.VMEM((2 * NCELL, 64, CT), jnp.bfloat16),
            pltpu.VMEM((blocks, BLOCK, 64), jnp.bfloat16),
            pltpu.VMEM((2 * NCELL, 8, BLOCK), F32),
            pltpu.VMEM((UNROLL, BLOCK, 2 * CT), jnp.bfloat16),
            pltpu.VMEM((UNROLL, BLOCK, BLOCK), F32),
            pltpu.VMEM((ITERS, 1, BLOCK), F32),
            pltpu.VMEM((ITERS, 1, BLOCK), F32),
            pltpu.VMEM((ITERS, segs, 1, BLOCK), F32),
            pltpu.VMEM((ITERS, lines, 1, BLOCK), F32),
            pltpu.SemaphoreType.DMA((ITERS,)),
            pltpu.SemaphoreType.DMA((ITERS,)),
            pltpu.SemaphoreType.DMA((ITERS,)),
            pltpu.SemaphoreType.DMA((ITERS, 2)),
            pltpu.SemaphoreType.DMA((ITERS,)),
        ],
        compiler_params=pltpu.CompilerParams(
            collective_id=1, has_side_effects=True, vmem_limit_bytes=VMEM_LIMIT
        ),
        name="em",
    )(src, near, near_pose, pose, cells)


def solution(mesh):
    lines, segs = mesh.shape["line"], mesh.shape["seg"]

    def on_device(points, rows, cells, pose):
        tiled = points.reshape(points.shape[2], points.shape[3] // BLOCK, BLOCK)
        pose_row = pose.reshape(1, 12)
        near, near_pose, src = fetch(tiled, rows[0, 0], pose_row, lines)
        matched, fitted, spread = em(src, near, near_pose, pose_row, cells[0, 0], lines, segs)
        return jnp.transpose(matched, (1, 0, 2))[None, None], fitted.reshape(12, 1), spread.reshape(1)

    return jax.shard_map(
        on_device,
        mesh=mesh,
        in_specs=(
            P("line", "seg", None, None),
            P("line", "seg", None, None),
            P("line", "seg", None, None),
            P(None, "line"),
        ),
        out_specs=(P("line", "seg", None, None, None), P(None, "line"), P()),
        check_vma=False,
    )
```

```python
import functools
import math

import jax
import jax.numpy as jnp
from jax import lax
from jax.experimental import pallas as pl
from jax.experimental.pallas import tpu as pltpu
from jax.sharding import PartitionSpec as P

NCELL = 16
CT = 512
BLOCK = 128
ITERS = 2
SPREAD_START = 0.05
PRIOR_TOP = 0.05
LOG2E = math.log2(math.e)
MARGIN = NCELL * CT
CHUNK = 16
UNROLL = 24
GATHER = 8
VMEM_LIMIT = 16 << 20
MESH = pl.DeviceIdType.MESH
F32 = jnp.float32


def iota(shape, dim):
    return lax.broadcasted_iota(jnp.int32, shape, dim)


def fetch_kernel(lines, points, row_lists, pose, near, near_pose, src, own, rows, own_sem, send_sem, recv_sem):
    me = lax.axis_index("line")
    upper, lower = lax.rem(me + 1, lines), lax.rem(me + lines - 1, lines)
    tiles = points.shape[1]
    margin_tiles = MARGIN // BLOCK
    low_tiles = pl.ds(0, margin_tiles)
    high_tiles = pl.ds(tiles - margin_tiles, margin_tiles)

    has_lower, has_upper = me > 0, me < lines - 1

    barrier = pltpu.get_barrier_semaphore()
    for peer in (lower, upper):
        pl.semaphore_signal(barrier, inc=1, device_id={"line": peer}, device_id_type=MESH)
    locals_ = [
        pltpu.make_async_copy(points.at[:, part], own.at[d], own_sem.at[d])
        for d, part in enumerate((low_tiles, high_tiles))
    ]
    row_copy = pltpu.make_async_copy(row_lists, rows, own_sem.at[2])
    row_copy.start()
    for copy in locals_:
        copy.start()

    def remote(source, target, slot, peer):
        return pltpu.make_async_remote_copy(
            src_ref=source,
            dst_ref=target,
            send_sem=send_sem.at[slot],
            recv_sem=recv_sem.at[slot],
            device_id={"line": peer},
            device_id_type=MESH,
        )

    up = [
        remote(points.at[:, high_tiles], near.at[0], 0, upper),
        remote(pose, near_pose.at[0], 2, upper),
    ]
    down = [
        remote(points.at[:, low_tiles], near.at[1], 1, lower),
        remote(pose, near_pose.at[1], 3, lower),
    ]

    for side, there in enumerate((has_lower, has_upper)):

        @pl.when(jnp.logical_not(there))
        def _():
            near[side] = jnp.zeros_like(near[side])
            near_pose[side] = jnp.zeros_like(near_pose[side])

    sub = iota((8, BLOCK), 0)
    blocks = rows.shape[1] // BLOCK

    def gather(d):
        @pl.loop(0, blocks // GATHER)
        def _(turn):
            for g in range(GATHER):
                b = turn * GATHER + g
                index = rows[d : d + 1, pl.ds(pl.multiple_of(b * BLOCK, BLOCK), BLOCK)]
                live = index >= 0
                local = index if d == 0 else index - (tiles * BLOCK - MARGIN)
                lane = jnp.broadcast_to(jnp.bitwise_and(local, 127), (8, BLOCK))
                high = jnp.broadcast_to(jnp.right_shift(local, 7), (8, BLOCK)) - sub
                found = [jnp.zeros((8, BLOCK), F32) for _ in range(3)]
                for u in range(margin_tiles // 8):
                    here = high == 8 * u
                    for k in range(3):
                        taken = jnp.take_along_axis(
                            own[d, k, 8 * u : 8 * u + 8, :], lane, axis=1, mode="promise_in_bounds"
                        )
                        found[k] = jnp.where(here, taken, found[k])
                alive = jnp.broadcast_to(live.astype(F32), (8, BLOCK))
                value = jnp.where(sub == 3, 1.0, jnp.where(sub == 4, alive, 0.0))
                for k in range(3):
                    picked = jnp.sum(found[k], axis=0, keepdims=True)
                    value = jnp.where(sub == k, jnp.broadcast_to(picked, (8, BLOCK)), value)
                src[d * blocks + b] = value

    pl.semaphore_wait(barrier, 2)

    for there, copies in ((has_upper, up), (has_lower, down)):

        @pl.when(there)
        def _():
            for copy in copies:
                copy.start()

    row_copy.wait()
    for d in range(2):
        locals_[d].wait()
        gather(d)
    for there, sent, received in ((has_upper, up, down), (has_lower, down, up)):

        @pl.when(there)
        def _():
            for copy in sent:
                copy.wait_send()
            for copy in received:
                copy.wait_recv()


def fetch(points, rows, pose, lines):
    blocks = rows.shape[0] * rows.shape[1] // BLOCK
    vmem = pl.BlockSpec(memory_space=pltpu.VMEM)
    return pl.pallas_call(
        functools.partial(fetch_kernel, lines),
        out_shape=(
            jax.ShapeDtypeStruct((2, 3, MARGIN // BLOCK, BLOCK), F32),
            jax.ShapeDtypeStruct((2, 1, 12), F32),
            jax.ShapeDtypeStruct((blocks, 8, BLOCK), F32),
        ),
        in_specs=[pl.BlockSpec(memory_space=pltpu.HBM)] * 3,
        out_specs=(vmem, vmem, vmem),
        scratch_shapes=[
            pltpu.VMEM((2, 3, MARGIN // BLOCK, BLOCK), F32),
            pltpu.VMEM(rows.shape, jnp.int32),
            pltpu.SemaphoreType.DMA((3,)),
            pltpu.SemaphoreType.DMA((4,)),
            pltpu.SemaphoreType.DMA((4,)),
        ],
        compiler_params=pltpu.CompilerParams(
            collective_id=0, has_side_effects=True, vmem_limit_bytes=VMEM_LIMIT
        ),
        name="fetch",
    )(points, rows, pose)


def pose_columns(row):
    sub = iota((8, BLOCK), 0)
    columns = []
    for c in range(4):
        value = jnp.zeros((8, BLOCK), F32)
        for k in range(3):
            lane = 3 * k + c if c < 3 else 9 + k
            value = jnp.where(sub == k, jnp.broadcast_to(row[:, lane : lane + 1], (8, BLOCK)), value)
        columns.append(value)
    return columns


def apply_pose(columns, coordinates):
    total = columns[3]
    for c in range(3):
        total = total + columns[c] * jnp.broadcast_to(coordinates[c], (8, BLOCK))
    return total


def split3(value):
    first = value.astype(jnp.bfloat16).astype(F32)
    rest = value - first
    second = rest.astype(jnp.bfloat16).astype(F32)
    return first, second, rest - second


def operand(value, norm_first):
    sub = iota((8, BLOCK), 0)
    norm = -jnp.sum(value * value, axis=0, keepdims=True)
    norms = [jnp.broadcast_to(part, (8, BLOCK)) for part in split3(norm)]
    if norm_first:
        value = 2.0 * value
        order = (0, 0, 0, 1, 1, 2, 1, 2)
        extra = norms + [1.0, 1.0, 1.0]
    else:
        order = (0, 1, 2, 0, 1, 0, 2, 1)
        extra = [1.0, 1.0, 1.0] + norms
    parts = split3(value)
    groups = [parts[p] for p in order]
    for i in range(6):
        groups[i] = jnp.where(sub == 3, extra[i], groups[i])
    return jnp.concatenate(groups, axis=0)


def em_kernel(
    lines, segs, src, near, near_pose, pose_in, cells_in, matched, fitted, final_spread,
    pose, cells, load_sem, side_y, side_m, centres, weights, energies, row_out, line_out, seg_in, line_in,
    seg_send, seg_recv, line_send, near_recv, line_recv,
):
    my_line, my_seg = lax.axis_index("line"), lax.axis_index("seg")
    blocks = src.shape[0] // 2
    tiles = CT // BLOCK
    sub = iota((8, BLOCK), 0)
    lanes = iota((8, BLOCK), 1)

    barrier = pltpu.get_barrier_semaphore()

    loads = [
        pltpu.make_async_copy(pose_in, pose, load_sem.at[0]),
        pltpu.make_async_copy(cells_in, cells, load_sem.at[1]),
    ]
    for copy in loads:
        copy.start()
    for k in range(1, segs):
        pl.semaphore_signal(
            barrier, inc=1, device_id={"seg": lax.rem(my_seg + k, segs)}, device_id_type=MESH
        )
    for k in range(1, lines):
        pl.semaphore_signal(
            barrier, inc=1, device_id={"line": lax.rem(my_line + k, lines)}, device_id_type=MESH
        )

    seg_order = sorted(range(1, segs), key=lambda k: -min(k, segs - k))
    line_order = [1, lines - 1] + sorted(range(2, lines - 1), key=lambda k: -min(k, lines - k))

    def seg_copy(it, k):
        return pltpu.make_async_remote_copy(
            src_ref=row_out.at[it],
            dst_ref=seg_in.at[it, my_seg],
            send_sem=seg_send.at[it],
            recv_sem=seg_recv.at[it],
            device_id={"seg": lax.rem(my_seg + k, segs)},
            device_id_type=MESH,
        )

    def line_copy(it, k):
        arrived = line_recv.at[it]
        if k == 1:
            arrived = near_recv.at[it, 0]
        elif k == lines - 1:
            arrived = near_recv.at[it, 1]
        return pltpu.make_async_remote_copy(
            src_ref=line_out.at[it],
            dst_ref=line_in.at[it, my_line],
            send_sem=line_send.at[it],
            recv_sem=arrived,
            device_id={"line": lax.rem(my_line + k, lines)},
            device_id_type=MESH,
        )

    def wait_rows(buffer, count, sem):
        part = buffer.at[pl.ds(0, count)]
        pltpu.make_async_copy(part, part, sem).wait()

    lower, upper = lax.rem(my_line + lines - 1, lines), lax.rem(my_line + 1, lines)

    low_pose = pose_columns(near_pose[0])
    up_pose = pose_columns(near_pose[1])
    spread = jnp.full((8, BLOCK), SPREAD_START, F32)

    def prepare_targets(low_pose, up_pose):
        for d in range(2):

            @pl.loop(0, NCELL)
            def _(c):
                world = []
                for t in range(tiles):
                    raw = [near[d, k, pl.ds(c * tiles + t, 1), :] for k in range(3)]
                    world.append(apply_pose((low_pose, up_pose)[d], raw))
                centre = world[0]
                for t in range(1, tiles):
                    centre = centre + world[t]
                centre = jnp.sum(centre, axis=1, keepdims=True) * (1.0 / CT)
                centre = jnp.broadcast_to(centre, (8, BLOCK))
                centres[d * NCELL + c] = centre
                for t in range(tiles):
                    here = slice(t * BLOCK, (t + 1) * BLOCK)
                    value = operand(world[t] - centre, False)
                    side_y[d * NCELL + c, :, here] = value.astype(jnp.bfloat16)

    def prepare_sources(own_pose):
        for d in range(2):

            @pl.loop(0, blocks // UNROLL)
            def _(turn):
                for u in range(UNROLL):
                    b = turn * UNROLL + u
                    x = src[d * blocks + b]
                    cell = jnp.maximum(cells[d, b], 0) + d * NCELL
                    moved = apply_pose(own_pose, [x[k : k + 1] for k in range(3)])
                    value = operand(moved - centres[cell], True)
                    side_m[d * blocks + b] = jnp.transpose(value).astype(jnp.bfloat16)

    prepare_targets(low_pose, up_pose)
    for copy in loads:
        copy.wait()
    own_pose = pose_columns(pose[...])
    prepare_sources(own_pose)
    for it in range(ITERS):
        last = it == ITERS - 1
        rate = LOG2E / (2.0 * spread)
        rate = jnp.concatenate([rate] * (CHUNK // 8), axis=0)
        rate = jnp.concatenate([rate] * tiles, axis=1)

        sums = [jnp.zeros((8, BLOCK), F32) for _ in range(7)]
        for d in range(2):

            def one_block(b, u, sums):
                x = src[d * blocks + b]
                cell = jnp.maximum(cells[d, b], 0) + d * NCELL
                exponents = jnp.dot(side_m[d * blocks + b], side_y[cell], preferred_element_type=F32)
                for i in range(BLOCK // CHUNK):
                    here = slice(i * CHUNK, (i + 1) * CHUNK)
                    exponent = exponents[here]
                    weight = lax.exp2(exponent * rate)
                    part = weight * exponent
                    energy = part[:, :BLOCK]
                    for t in range(1, tiles):
                        energy = energy + part[:, t * BLOCK : (t + 1) * BLOCK]
                    energies[u, here, :] = energy
                    high = weight.astype(jnp.bfloat16)
                    weights[u, here, :] = high
                    weights[u, BLOCK + i * CHUNK : BLOCK + (i + 1) * CHUNK, :] = (
                        weight - high.astype(F32)
                    ).astype(jnp.bfloat16)
                out = lax.dot_general(
                    weights[u],
                    side_y[cell, 0:32, :],
                    (((1,), (1,)), ((), ())),
                    preferred_element_type=F32,
                )
                out = jnp.transpose(out[:BLOCK] + out[BLOCK:])
                pulled = out[0:8] + jnp.where(sub == 3, 0.0, out[8:16] + out[16:24])
                energy = jnp.sum(jnp.transpose(energies[u]), axis=0, keepdims=True)
                total = jnp.broadcast_to(pulled[3:4], (8, BLOCK))
                factor = jnp.broadcast_to(x[4:5], (8, BLOCK)) / (total + 1.0)
                merged = jnp.where(sub == 4, jnp.broadcast_to(-energy, (8, BLOCK)), pulled)
                result = (merged + centres[cell] * total) * factor
                if last:
                    here = pl.ds(pl.multiple_of(b * BLOCK, BLOCK), BLOCK)
                    for k in range(5):
                        matched[k, d : d + 1, here] = result[k : k + 1]
                share = jnp.broadcast_to(result[3:4], (8, BLOCK))
                weighted = share * x
                new = []
                for c in range(4):
                    new.append(sums[c] + (result * jnp.broadcast_to(x[c : c + 1], (8, BLOCK)) if c < 3 else result))
                for c in range(3):
                    new.append(sums[4 + c] + weighted * jnp.broadcast_to(x[c : c + 1], (8, BLOCK)))
                return tuple(new)

            def some_blocks(turn, sums):
                for u in range(UNROLL):
                    sums = one_block(turn * UNROLL + u, u, sums)
                return sums

            sums = lax.fori_loop(0, blocks // UNROLL, some_blocks, tuple(sums))

        row = jnp.zeros((8, BLOCK), F32)
        for q in range(7):
            column = jnp.sum(sums[q], axis=1, keepdims=True)
            row = row + jnp.where(lanes == 8 * q + sub, jnp.broadcast_to(column, (8, BLOCK)), 0.0)
        row = jnp.sum(row, axis=0, keepdims=True)
        row_out[it] = row
        seg_in[it, my_seg] = row
        if it == 0:
            pl.semaphore_wait(barrier, segs + lines - 2)
        for k in seg_order:
            seg_copy(it, k).start()

        kept = jnp.zeros((8, BLOCK), F32)
        for c in range(4):
            kept = kept + jnp.where((lanes == 64 + 8 * c + sub) & (sub < 3), own_pose[c], 0.0)
        kept = jnp.sum(kept, axis=0, keepdims=True)

        wait_rows(seg_in.at[it], segs - 1, seg_recv.at[it])
        line_row = kept + jnp.sum(seg_in[it], axis=0)
        line_out[it] = line_row
        line_in[it, my_line] = line_row
        for k in line_order:
            line_copy(it, k).start()
        wait_rows(seg_in.at[it], segs - 1, seg_send.at[it])
        for k in range(2):
            wait_rows(line_in.at[it], 1, near_recv.at[it, k])

        three = jnp.where(sub == 0, line_in[it, lower], jnp.where(sub == 1, line_row, line_in[it, upper]))
        turned = jnp.transpose(three)
        part = [jnp.concatenate([turned[8 * q : 8 * q + 8], jnp.zeros((8, BLOCK - 8), F32)], axis=1) for q in range(12)]

        def entry(q, r):
            return jnp.broadcast_to(part[q][r : r + 1], (8, BLOCK))

        n = [[None] * 4 for _ in range(4)]
        for a in range(3):
            for c in range(a + 1):
                n[a][c] = entry(4 + c, a)
        for c in range(4):
            n[3][c] = entry(c, 3)
        for a in range(4):
            n[a][a] = n[a][a] + 1.0
        low = [[None] * 4 for _ in range(4)]
        inverse = [None] * 4
        for c in range(4):
            diagonal = n[c][c]
            for j in range(c):
                diagonal = diagonal - low[c][j] * n[c][j]
            inverse[c] = 1.0 / diagonal
            for a in range(c + 1, 4):
                for j in range(c):
                    n[a][c] = n[a][c] - low[c][j] * n[a][j]
                low[a][c] = n[a][c] * inverse[c]
        z = [part[c] + part[8 + c] for c in range(4)]
        for a in range(4):
            for c in range(a):
                z[a] = z[a] - low[a][c] * z[c]
        z = [z[a] * inverse[a] for a in range(4)]
        for a in range(3, -1, -1):
            for c in range(a + 1, 4):
                z[a] = z[a] - low[c][a] * z[c]

        def pick(which):
            columns = []
            for c in range(4):
                value = jnp.sum(jnp.where((lanes == which) & (sub < 3), z[c], 0.0), axis=1, keepdims=True)
                columns.append(jnp.broadcast_to(value, (8, BLOCK)))
            return columns

        own_pose = pick(1)
        if not last:
            low_pose, up_pose = pick(0), pick(2)
            prepare_targets(low_pose, up_pose)
            prepare_sources(own_pose)
        wait_rows(line_in.at[it], lines - 3, line_recv.at[it])
        totals = jnp.sum(line_in[it], axis=0)
        spread = (totals[:, 28:29] + PRIOR_TOP) / (3.0 * totals[:, 27:28] + 1.0)
        spread = jnp.broadcast_to(spread, (8, BLOCK))
        wait_rows(line_in.at[it], lines - 1, line_send.at[it])

    line = jnp.zeros((8, BLOCK), F32)
    for c in range(4):
        lane = 3 * sub + c if c < 3 else 9 + sub
        line = line + jnp.where((lanes == lane) & (sub < 3), own_pose[c], 0.0)
    fitted[...] = jnp.sum(line, axis=0, keepdims=True)[:, 0:12]
    final_spread[...] = spread[0:1, 0:1]


def em(src, near, near_pose, pose, cells, lines, segs):
    blocks = src.shape[0]
    vmem = pl.BlockSpec(memory_space=pltpu.VMEM)
    hbm = pl.BlockSpec(memory_space=pltpu.HBM)
    return pl.pallas_call(
        functools.partial(em_kernel, lines, segs),
        out_shape=(
            jax.ShapeDtypeStruct((5, 2, blocks // 2 * BLOCK), F32),
            jax.ShapeDtypeStruct((1, 12), F32),
            jax.ShapeDtypeStruct((1, 1), F32),
        ),
        in_specs=[vmem, vmem, vmem, hbm, hbm],
        out_specs=(vmem, vmem, vmem),
        scratch_shapes=[
            pltpu.VMEM(pose.shape, F32),
            pltpu.SMEM(cells.shape, jnp.int32),
            pltpu.SemaphoreType.DMA((2,)),
            pltpu.VMEM((2 * NCELL, 64, CT), jnp.bfloat16),
            pltpu.VMEM((blocks, BLOCK, 64), jnp.bfloat16),
            pltpu.VMEM((2 * NCELL, 8, BLOCK), F32),
            pltpu.VMEM((UNROLL, 2 * BLOCK, CT), jnp.bfloat16),
            pltpu.VMEM((UNROLL, BLOCK, BLOCK), F32),
            pltpu.VMEM((ITERS, 1, BLOCK), F32),
            pltpu.VMEM((ITERS, 1, BLOCK), F32),
            pltpu.VMEM((ITERS, segs, 1, BLOCK), F32),
            pltpu.VMEM((ITERS, lines, 1, BLOCK), F32),
            pltpu.SemaphoreType.DMA((ITERS,)),
            pltpu.SemaphoreType.DMA((ITERS,)),
            pltpu.SemaphoreType.DMA((ITERS,)),
            pltpu.SemaphoreType.DMA((ITERS, 2)),
            pltpu.SemaphoreType.DMA((ITERS,)),
        ],
        compiler_params=pltpu.CompilerParams(
            collective_id=1, has_side_effects=True, vmem_limit_bytes=VMEM_LIMIT
        ),
        name="em",
    )(src, near, near_pose, pose, cells)


def solution(mesh):
    lines, segs = mesh.shape["line"], mesh.shape["seg"]

    def on_device(points, rows, cells, pose):
        tiled = points.reshape(points.shape[2], points.shape[3] // BLOCK, BLOCK)
        pose_row = pose.reshape(1, 12)
        tiled, row_lists, pose_row, cell_lists = (
            pltpu.with_memory_space_constraint(value, pltpu.HBM)
            for value in (tiled, rows[0, 0], pose_row, cells[0, 0])
        )
        near, near_pose, src = fetch(tiled, row_lists, pose_row, lines)
        matched, fitted, spread = em(src, near, near_pose, pose_row, cell_lists, lines, segs)
        return jnp.transpose(matched, (1, 0, 2))[None, None], fitted.reshape(12, 1), spread.reshape(1)

    return jax.shard_map(
        on_device,
        mesh=mesh,
        in_specs=(
            P("line", "seg", None, None),
            P("line", "seg", None, None),
            P("line", "seg", None, None),
            P(None, "line"),
        ),
        out_specs=(P("line", "seg", None, None, None), P(None, "line"), P()),
        check_vma=False,
    )
```

```python
import functools
import math

import jax
import jax.numpy as jnp
from jax import lax
from jax.experimental import pallas as pl
from jax.experimental.pallas import tpu as pltpu
from jax.sharding import PartitionSpec as P

NCELL = 16
CT = 512
BLOCK = 128
ITERS = 2
SPREAD_START = 0.05
PRIOR_TOP = 0.05
LOG2E = math.log2(math.e)
MARGIN = NCELL * CT
CHUNK = 16
UNROLL = 24
GATHER = 8
VMEM_LIMIT = 16 << 20
MESH = pl.DeviceIdType.MESH
F32 = jnp.float32


def iota(shape, dim):
    return lax.broadcasted_iota(jnp.int32, shape, dim)


def fetch_kernel(lines, points, row_lists, pose, near, near_pose, src, own, rows, own_sem, send_sem, recv_sem):
    me = lax.axis_index("line")
    upper, lower = lax.rem(me + 1, lines), lax.rem(me + lines - 1, lines)
    tiles = points.shape[1]
    margin_tiles = MARGIN // BLOCK
    low_tiles = pl.ds(0, margin_tiles)
    high_tiles = pl.ds(tiles - margin_tiles, margin_tiles)

    has_lower, has_upper = me > 0, me < lines - 1

    barrier = pltpu.get_barrier_semaphore()
    for peer in (lower, upper):
        pl.semaphore_signal(barrier, inc=1, device_id={"line": peer}, device_id_type=MESH)
    locals_ = [
        pltpu.make_async_copy(points.at[:, part], own.at[d], own_sem.at[d])
        for d, part in enumerate((low_tiles, high_tiles))
    ]
    row_copy = pltpu.make_async_copy(row_lists, rows, own_sem.at[2])
    row_copy.start()
    for copy in locals_:
        copy.start()

    def remote(source, target, slot, peer):
        return pltpu.make_async_remote_copy(
            src_ref=source,
            dst_ref=target,
            send_sem=send_sem.at[slot],
            recv_sem=recv_sem.at[slot],
            device_id={"line": peer},
            device_id_type=MESH,
        )

    up = [
        remote(points.at[:, high_tiles], near.at[0], 0, upper),
        remote(pose, near_pose.at[0], 2, upper),
    ]
    down = [
        remote(points.at[:, low_tiles], near.at[1], 1, lower),
        remote(pose, near_pose.at[1], 3, lower),
    ]

    for side, there in enumerate((has_lower, has_upper)):

        @pl.when(jnp.logical_not(there))
        def _():
            near[side] = jnp.zeros_like(near[side])
            near_pose[side] = jnp.zeros_like(near_pose[side])

    sub = iota((8, BLOCK), 0)
    blocks = rows.shape[1] // BLOCK

    def gather(d):
        @pl.loop(0, blocks // GATHER)
        def _(turn):
            for g in range(GATHER):
                b = turn * GATHER + g
                index = rows[d : d + 1, pl.ds(pl.multiple_of(b * BLOCK, BLOCK), BLOCK)]
                live = index >= 0
                local = index if d == 0 else index - (tiles * BLOCK - MARGIN)
                lane = jnp.broadcast_to(jnp.bitwise_and(local, 127), (8, BLOCK))
                high = jnp.broadcast_to(jnp.right_shift(local, 7), (8, BLOCK)) - sub
                found = [jnp.zeros((8, BLOCK), F32) for _ in range(3)]
                for u in range(margin_tiles // 8):
                    here = high == 8 * u
                    for k in range(3):
                        taken = jnp.take_along_axis(
                            own[d, k, 8 * u : 8 * u + 8, :], lane, axis=1, mode="promise_in_bounds"
                        )
                        found[k] = jnp.where(here, taken, found[k])
                alive = jnp.broadcast_to(live.astype(F32), (8, BLOCK))
                value = jnp.where(sub == 3, 1.0, jnp.where(sub == 4, alive, 0.0))
                for k in range(3):
                    picked = jnp.sum(found[k], axis=0, keepdims=True)
                    value = jnp.where(sub == k, jnp.broadcast_to(picked, (8, BLOCK)), value)
                src[d * blocks + b] = value

    pl.semaphore_wait(barrier, 2)

    for there, copies in ((has_upper, up), (has_lower, down)):

        @pl.when(there)
        def _():
            for copy in copies:
                copy.start()

    row_copy.wait()
    for d in range(2):
        locals_[d].wait()
        gather(d)
    for there, sent, received in ((has_upper, up, down), (has_lower, down, up)):

        @pl.when(there)
        def _():
            for copy in sent:
                copy.wait_send()
            for copy in received:
                copy.wait_recv()


def fetch(points, rows, pose, lines):
    blocks = rows.shape[0] * rows.shape[1] // BLOCK
    vmem = pl.BlockSpec(memory_space=pltpu.VMEM)
    return pl.pallas_call(
        functools.partial(fetch_kernel, lines),
        out_shape=(
            jax.ShapeDtypeStruct((2, 3, MARGIN // BLOCK, BLOCK), F32),
            jax.ShapeDtypeStruct((2, 1, 12), F32),
            jax.ShapeDtypeStruct((blocks, 8, BLOCK), F32),
        ),
        in_specs=[pl.BlockSpec(memory_space=pltpu.HBM)] * 3,
        out_specs=(vmem, vmem, vmem),
        scratch_shapes=[
            pltpu.VMEM((2, 3, MARGIN // BLOCK, BLOCK), F32),
            pltpu.VMEM(rows.shape, jnp.int32),
            pltpu.SemaphoreType.DMA((3,)),
            pltpu.SemaphoreType.DMA((4,)),
            pltpu.SemaphoreType.DMA((4,)),
        ],
        compiler_params=pltpu.CompilerParams(
            collective_id=0, has_side_effects=True, vmem_limit_bytes=VMEM_LIMIT
        ),
        name="fetch",
    )(points, rows, pose)


def pose_columns(row):
    sub = iota((8, BLOCK), 0)
    columns = []
    for c in range(4):
        value = jnp.zeros((8, BLOCK), F32)
        for k in range(3):
            lane = 3 * k + c if c < 3 else 9 + k
            value = jnp.where(sub == k, jnp.broadcast_to(row[:, lane : lane + 1], (8, BLOCK)), value)
        columns.append(value)
    return columns


def apply_pose(columns, coordinates):
    total = columns[3]
    for c in range(3):
        total = total + columns[c] * jnp.broadcast_to(coordinates[c], (8, BLOCK))
    return total


def split3(value):
    first = value.astype(jnp.bfloat16).astype(F32)
    rest = value - first
    second = rest.astype(jnp.bfloat16).astype(F32)
    return first, second, rest - second


def operand(value, norm_first):
    sub = iota((8, BLOCK), 0)
    norm = -jnp.sum(value * value, axis=0, keepdims=True)
    norms = [jnp.broadcast_to(part, (8, BLOCK)) for part in split3(norm)]
    if norm_first:
        value = 2.0 * value
        order = (0, 0, 0, 1, 1, 2, 1, 2)
        extra = norms + [1.0, 1.0, 1.0]
    else:
        order = (0, 1, 2, 0, 1, 0, 2, 1)
        extra = [1.0, 1.0, 1.0] + norms
    parts = split3(value)
    groups = [parts[p] for p in order]
    for i in range(6):
        groups[i] = jnp.where(sub == 3, extra[i], groups[i])
    return jnp.concatenate(groups, axis=0)


def em_kernel(
    lines, segs, src, near, near_pose, pose_in, cells_in, matched, fitted, final_spread,
    pose, cells, load_sem, side_y, side_m, centres, weights, energies, row_out, line_out, seg_in, line_in,
    seg_send, seg_recv, line_send, near_recv, line_recv,
):
    my_line, my_seg = lax.axis_index("line"), lax.axis_index("seg")
    blocks = src.shape[0] // 2
    tiles = CT // BLOCK
    sub = iota((8, BLOCK), 0)
    lanes = iota((8, BLOCK), 1)

    barrier = pltpu.get_barrier_semaphore()

    loads = [
        pltpu.make_async_copy(pose_in, pose, load_sem.at[0]),
        pltpu.make_async_copy(cells_in, cells, load_sem.at[1]),
    ]
    for copy in loads:
        copy.start()
    for k in range(1, segs):
        pl.semaphore_signal(
            barrier, inc=1, device_id={"seg": lax.rem(my_seg + k, segs)}, device_id_type=MESH
        )
    for k in range(1, lines):
        pl.semaphore_signal(
            barrier, inc=1, device_id={"line": lax.rem(my_line + k, lines)}, device_id_type=MESH
        )

    seg_order = sorted(range(1, segs), key=lambda k: -min(k, segs - k))
    line_order = [1, lines - 1] + sorted(range(2, lines - 1), key=lambda k: -min(k, lines - k))

    def seg_copy(it, k):
        return pltpu.make_async_remote_copy(
            src_ref=row_out.at[it],
            dst_ref=seg_in.at[it, my_seg],
            send_sem=seg_send.at[it],
            recv_sem=seg_recv.at[it],
            device_id={"seg": lax.rem(my_seg + k, segs)},
            device_id_type=MESH,
        )

    def line_copy(it, k):
        arrived = line_recv.at[it]
        if k == 1:
            arrived = near_recv.at[it, 0]
        elif k == lines - 1:
            arrived = near_recv.at[it, 1]
        return pltpu.make_async_remote_copy(
            src_ref=line_out.at[it],
            dst_ref=line_in.at[it, my_line],
            send_sem=line_send.at[it],
            recv_sem=arrived,
            device_id={"line": lax.rem(my_line + k, lines)},
            device_id_type=MESH,
        )

    def wait_rows(buffer, count, sem):
        part = buffer.at[pl.ds(0, count)]
        pltpu.make_async_copy(part, part, sem).wait()

    lower, upper = lax.rem(my_line + lines - 1, lines), lax.rem(my_line + 1, lines)

    low_pose = pose_columns(near_pose[0])
    up_pose = pose_columns(near_pose[1])
    spread = jnp.full((8, BLOCK), SPREAD_START, F32)

    def prepare_targets(low_pose, up_pose):
        @pl.loop(0, NCELL)
        def _(c):
            for d in range(2):
                world = []
                for t in range(tiles):
                    raw = [near[d, k, pl.ds(c * tiles + t, 1), :] for k in range(3)]
                    world.append(apply_pose((low_pose, up_pose)[d], raw))
                centre = world[0]
                for t in range(1, tiles):
                    centre = centre + world[t]
                centre = jnp.sum(centre, axis=1, keepdims=True) * (1.0 / CT)
                centre = jnp.broadcast_to(centre, (8, BLOCK))
                centres[d * NCELL + c] = centre
                for t in range(tiles):
                    here = slice(t * BLOCK, (t + 1) * BLOCK)
                    value = operand(world[t] - centre, False)
                    side_y[d * NCELL + c, :, here] = value.astype(jnp.bfloat16)

    def prepare_sources(own_pose):
        for d in range(2):

            @pl.loop(0, blocks // UNROLL)
            def _(turn):
                for u in range(UNROLL):
                    b = turn * UNROLL + u
                    x = src[d * blocks + b]
                    cell = jnp.maximum(cells[d, b], 0) + d * NCELL
                    moved = apply_pose(own_pose, [x[k : k + 1] for k in range(3)])
                    value = operand(moved - centres[cell], True)
                    side_m[d * blocks + b] = jnp.transpose(value).astype(jnp.bfloat16)

    prepare_targets(low_pose, up_pose)
    for copy in loads:
        copy.wait()
    own_pose = pose_columns(pose[...])
    prepare_sources(own_pose)
    for it in range(ITERS):
        last = it == ITERS - 1
        rate = LOG2E / (2.0 * spread)
        rate = jnp.concatenate([rate] * (CHUNK // 8), axis=0)
        rate = jnp.concatenate([rate] * tiles, axis=1)

        sums = [jnp.zeros((8, BLOCK), F32) for _ in range(7)]
        for d in range(2):

            def one_block(b, u, sums):
                x = src[d * blocks + b]
                cell = jnp.maximum(cells[d, b], 0) + d * NCELL
                exponents = jnp.dot(side_m[d * blocks + b], side_y[cell], preferred_element_type=F32)
                for i in range(BLOCK // CHUNK):
                    here = slice(i * CHUNK, (i + 1) * CHUNK)
                    exponent = exponents[here]
                    weight = lax.exp2(exponent * rate)
                    part = weight * exponent
                    energy = part[:, :BLOCK]
                    for t in range(1, tiles):
                        energy = energy + part[:, t * BLOCK : (t + 1) * BLOCK]
                    energies[u, here, :] = energy
                    high = weight.astype(jnp.bfloat16)
                    weights[u, here, :] = high
                    weights[u, BLOCK + i * CHUNK : BLOCK + (i + 1) * CHUNK, :] = (
                        weight - high.astype(F32)
                    ).astype(jnp.bfloat16)
                out = lax.dot_general(
                    weights[u],
                    side_y[cell, 0:32, :],
                    (((1,), (1,)), ((), ())),
                    preferred_element_type=F32,
                )
                out = jnp.transpose(out[:BLOCK] + out[BLOCK:])
                pulled = out[0:8] + jnp.where(sub == 3, 0.0, out[8:16] + out[16:24])
                energy = jnp.sum(jnp.transpose(energies[u]), axis=0, keepdims=True)
                total = jnp.broadcast_to(pulled[3:4], (8, BLOCK))
                factor = jnp.broadcast_to(x[4:5], (8, BLOCK)) / (total + 1.0)
                merged = jnp.where(sub == 4, jnp.broadcast_to(-energy, (8, BLOCK)), pulled)
                result = (merged + centres[cell] * total) * factor
                if last:
                    here = pl.ds(pl.multiple_of(b * BLOCK, BLOCK), BLOCK)
                    for k in range(5):
                        matched[k, d : d + 1, here] = result[k : k + 1]
                share = jnp.broadcast_to(result[3:4], (8, BLOCK))
                weighted = share * x
                new = []
                for c in range(4):
                    new.append(sums[c] + (result * jnp.broadcast_to(x[c : c + 1], (8, BLOCK)) if c < 3 else result))
                for c in range(3):
                    new.append(sums[4 + c] + weighted * jnp.broadcast_to(x[c : c + 1], (8, BLOCK)))
                return tuple(new)

            def some_blocks(turn, sums):
                for u in range(UNROLL):
                    sums = one_block(turn * UNROLL + u, u, sums)
                return sums

            sums = lax.fori_loop(0, blocks // UNROLL, some_blocks, tuple(sums))

        row = jnp.zeros((8, BLOCK), F32)
        for q in range(7):
            column = jnp.sum(sums[q], axis=1, keepdims=True)
            row = row + jnp.where(lanes == 8 * q + sub, jnp.broadcast_to(column, (8, BLOCK)), 0.0)
        row = jnp.sum(row, axis=0, keepdims=True)
        row_out[it] = row
        seg_in[it, my_seg] = row
        if it == 0:
            pl.semaphore_wait(barrier, segs + lines - 2)
        for k in seg_order:
            seg_copy(it, k).start()

        kept = jnp.zeros((8, BLOCK), F32)
        for c in range(4):
            kept = kept + jnp.where((lanes == 64 + 8 * c + sub) & (sub < 3), own_pose[c], 0.0)
        kept = jnp.sum(kept, axis=0, keepdims=True)

        wait_rows(seg_in.at[it], segs - 1, seg_recv.at[it])
        line_row = kept + jnp.sum(seg_in[it], axis=0)
        line_out[it] = line_row
        line_in[it, my_line] = line_row
        for k in line_order:
            line_copy(it, k).start()
        wait_rows(seg_in.at[it], segs - 1, seg_send.at[it])
        for k in range(2):
            wait_rows(line_in.at[it], 1, near_recv.at[it, k])

        three = jnp.where(sub == 0, line_in[it, lower], jnp.where(sub == 1, line_row, line_in[it, upper]))
        turned = jnp.transpose(three)
        part = [jnp.concatenate([turned[8 * q : 8 * q + 8], jnp.zeros((8, BLOCK - 8), F32)], axis=1) for q in range(12)]

        def entry(q, r):
            return jnp.broadcast_to(part[q][r : r + 1], (8, BLOCK))

        n = [[None] * 4 for _ in range(4)]
        for a in range(3):
            for c in range(a + 1):
                n[a][c] = entry(4 + c, a)
        for c in range(4):
            n[3][c] = entry(c, 3)
        for a in range(4):
            n[a][a] = n[a][a] + 1.0
        low = [[None] * 4 for _ in range(4)]
        inverse = [None] * 4
        for c in range(4):
            diagonal = n[c][c]
            for j in range(c):
                diagonal = diagonal - low[c][j] * n[c][j]
            inverse[c] = 1.0 / diagonal
            for a in range(c + 1, 4):
                for j in range(c):
                    n[a][c] = n[a][c] - low[c][j] * n[a][j]
                low[a][c] = n[a][c] * inverse[c]
        z = [part[c] + part[8 + c] for c in range(4)]
        for a in range(4):
            for c in range(a):
                z[a] = z[a] - low[a][c] * z[c]
        z = [z[a] * inverse[a] for a in range(4)]
        for a in range(3, -1, -1):
            for c in range(a + 1, 4):
                z[a] = z[a] - low[c][a] * z[c]

        def pick(which):
            columns = []
            for c in range(4):
                value = jnp.sum(jnp.where((lanes == which) & (sub < 3), z[c], 0.0), axis=1, keepdims=True)
                columns.append(jnp.broadcast_to(value, (8, BLOCK)))
            return columns

        own_pose = pick(1)
        if not last:
            low_pose, up_pose = pick(0), pick(2)
            prepare_targets(low_pose, up_pose)
            prepare_sources(own_pose)
        wait_rows(line_in.at[it], lines - 3, line_recv.at[it])
        totals = jnp.sum(line_in[it], axis=0)
        spread = (totals[:, 28:29] + PRIOR_TOP) / (3.0 * totals[:, 27:28] + 1.0)
        spread = jnp.broadcast_to(spread, (8, BLOCK))
        wait_rows(line_in.at[it], lines - 1, line_send.at[it])

    line = jnp.zeros((8, BLOCK), F32)
    for c in range(4):
        lane = 3 * sub + c if c < 3 else 9 + sub
        line = line + jnp.where((lanes == lane) & (sub < 3), own_pose[c], 0.0)
    fitted[...] = jnp.sum(line, axis=0, keepdims=True)[:, 0:12]
    final_spread[...] = spread[0:1, 0:1]


def em(src, near, near_pose, pose, cells, lines, segs):
    blocks = src.shape[0]
    vmem = pl.BlockSpec(memory_space=pltpu.VMEM)
    hbm = pl.BlockSpec(memory_space=pltpu.HBM)
    return pl.pallas_call(
        functools.partial(em_kernel, lines, segs),
        out_shape=(
            jax.ShapeDtypeStruct((5, 2, blocks // 2 * BLOCK), F32),
            jax.ShapeDtypeStruct((1, 12), F32),
            jax.ShapeDtypeStruct((1, 1), F32),
        ),
        in_specs=[vmem, vmem, vmem, hbm, hbm],
        out_specs=(vmem, vmem, vmem),
        scratch_shapes=[
            pltpu.VMEM(pose.shape, F32),
            pltpu.SMEM(cells.shape, jnp.int32),
            pltpu.SemaphoreType.DMA((2,)),
            pltpu.VMEM((2 * NCELL, 64, CT), jnp.bfloat16),
            pltpu.VMEM((blocks, BLOCK, 64), jnp.bfloat16),
            pltpu.VMEM((2 * NCELL, 8, BLOCK), F32),
            pltpu.VMEM((UNROLL, 2 * BLOCK, CT), jnp.bfloat16),
            pltpu.VMEM((UNROLL, BLOCK, BLOCK), F32),
            pltpu.VMEM((ITERS, 1, BLOCK), F32),
            pltpu.VMEM((ITERS, 1, BLOCK), F32),
            pltpu.VMEM((ITERS, segs, 1, BLOCK), F32),
            pltpu.VMEM((ITERS, lines, 1, BLOCK), F32),
            pltpu.SemaphoreType.DMA((ITERS,)),
            pltpu.SemaphoreType.DMA((ITERS,)),
            pltpu.SemaphoreType.DMA((ITERS,)),
            pltpu.SemaphoreType.DMA((ITERS, 2)),
            pltpu.SemaphoreType.DMA((ITERS,)),
        ],
        compiler_params=pltpu.CompilerParams(
            collective_id=1,
            has_side_effects=True,
            vmem_limit_bytes=VMEM_LIMIT,
        ),
        name="em",
    )(src, near, near_pose, pose, cells)


def solution(mesh):
    lines, segs = mesh.shape["line"], mesh.shape["seg"]

    def on_device(points, rows, cells, pose):
        tiled = points.reshape(points.shape[2], points.shape[3] // BLOCK, BLOCK)
        pose_row = pose.reshape(1, 12)
        tiled, row_lists, pose_row, cell_lists = (
            pltpu.with_memory_space_constraint(value, pltpu.HBM)
            for value in (tiled, rows[0, 0], pose_row, cells[0, 0])
        )
        near, near_pose, src = fetch(tiled, row_lists, pose_row, lines)
        matched, fitted, spread = em(src, near, near_pose, pose_row, cell_lists, lines, segs)
        return jnp.transpose(matched, (1, 0, 2))[None, None], fitted.reshape(12, 1), spread.reshape(1)

    return jax.shard_map(
        on_device,
        mesh=mesh,
        in_specs=(
            P("line", "seg", None, None),
            P("line", "seg", None, None),
            P("line", "seg", None, None),
            P(None, "line"),
        ),
        out_specs=(P("line", "seg", None, None, None), P(None, "line"), P()),
        check_vma=False,
    )
```
